32 devices in a mesh: pair: 4 (over y, core), fold: 8 (over z, x).
Axes of the slice: x: 2, y: 2, z: 4, core: 2. Of those that a mesh axis runs over, the one named last changes fastest.
Arguments:
- amplitudes: bfloat16 [4, 80, 640, 640], P(None, 'pair', 'fold'), may hold values from -6 to 6
- cycle_block: bfloat16 [640, 80, 8, 640], P('fold', None, 'pair'), may hold values from -0.078125 to 0.078125
- occ_sizes: int32 [8], replicated, may hold values from 1 to 20, 80 in all
- vir_sizes: int32 [8], replicated, may hold values from 1 to 160, 640 in all
- window_i: int32 [4], replicated, may hold values from 0 to 79
- window_occ: int32 [8], replicated, may hold values from 0 to 79
Outputs:
- residual: bfloat16 [4, 640, 8, 640], P(None, 'fold', 'pair')
The draws below stay inside these ranges and needn't reach their ends.
Inputs may be any that keep to these rules, and one draw needn't show every extreme that they name: `occ_sizes`: the entries sum to 80. `vir_sizes`: the entries sum to 640.
All inputs are finite; a program needn't handle non-finite values.
Results may differ from the reference program's by a relative error of at most 0.001.
Values may be sent and summed in bfloat16 or wider, within the bound.
A program may use at most 128 MiB of HBM per device.

```python
import math
import jax
import jax.numpy as jnp
import numpy as np
from jax import lax

V = 640
NK = 80
NI = 4
NJ = 8
IRREPS = 8


def with_ends(values, key, least, top_value):
    longest = values.shape.index(max(values.shape))
    spots = []
    for shift in (0, 1):
        where = [jax.random.randint(jax.random.fold_in(key, axis), (), 0, length) for axis, length in enumerate(values.shape)]
        where[longest] = (where[longest] + shift) % values.shape[longest]
        spots.append(tuple(where))
    return values.at[spots[0]].set(least).at[spots[1]].set(top_value)


def spiked(array, stream_key, source, target, blocks, factor):
    def block_of(dim):
        return (jnp.arange(array.shape[dim]) // (array.shape[dim] // blocks)).reshape((-1,) + (1,) * (array.ndim - 1 - dim))

    first = jax.random.permutation(stream_key, blocks)[block_of(target)]
    other_side = (block_of(target) + blocks // 2) % blocks
    return jnp.where((block_of(source) == first) | (block_of(source) == other_side), factor * array, array)


def shard_levels(own_key, shape, pieces, least, top_value):
    def one(position, parts):
        steps = jax.random.uniform(jax.random.fold_in(jax.random.fold_in(own_key, 6), position), (parts,), jnp.float32, least / len(pieces), top_value / len(pieces))
        return jnp.repeat(jnp.exp(steps), shape[position] // parts).reshape((-1,) + (1,) * (len(shape) - position - 1))

    factor_of = one(*pieces[0])
    for cut in pieces[1:]:
        factor_of = factor_of * one(*cut)
    return factor_of


def length_profile(amount, total, bound, slope):
    loads = [(1 << 20) // math.isqrt(grade ** slope) + 1 for grade in range(2, amount + 1)]
    spare, counts = total - bound - (amount - 1), [1] * (amount - 1)
    while spare > 0:
        free = [i for i in range(amount - 1) if counts[i] < bound]
        whole, remaining = sum([loads[i] for i in free]), spare
        for i in free:
            extra = min(bound - counts[i], max(1, remaining * loads[i] // whole), spare)
            counts[i] = counts[i] + extra
            spare = spare - extra
    return np.array([bound] + counts)


def uneven(rng, amount, total, limit, slope):
    if amount == 2:
        one = jax.random.randint(rng, (), max(1, total - limit), min(limit, total - 1) + 1)
        return jnp.stack([one, total - one])
    tallies = jnp.asarray(length_profile(amount, total, limit, slope), jnp.int32)
    pairs = (amount - 1) // 2
    giver, sink = tallies[1:1 + 2 * pairs:2], tallies[2:2 + 2 * pairs:2]
    slack = jnp.minimum(giver - 1, limit - sink)
    shifted = jax.random.randint(jax.random.fold_in(rng, 1), (pairs,), 0, 1 << 20) % (slack + 1)
    tallies = tallies.at[1:1 + 2 * pairs:2].set(giver - shifted).at[2:2 + 2 * pairs:2].set(sink + shifted)
    return tallies[jax.random.permutation(jax.random.fold_in(rng, 2), amount)]


def centred(own_key, dims, width, most, shards=(), kind=jnp.bfloat16):
    values = width * jax.random.normal(own_key, dims, jnp.float32)
    if shards:
        values = values * shard_levels(own_key, dims, shards, -0.22, 0.18)
    return jnp.clip(values, -most, most).astype(kind)


def noise_with(key, shape, deviation, reach, cuts, heavy, kind=jnp.bfloat16):
    drawn = deviation * jax.random.normal(key, shape, jnp.float32)
    if cuts:
        drawn = drawn * shard_levels(key, shape, cuts, -0.22, 0.18)
    return jnp.clip(spiked(drawn, jax.random.fold_in(key, 3), *heavy), -reach, reach).astype(kind)


def setup_inputs(seed: int = 0) -> dict:
    key_of = jax.random.split(jax.random.key(seed), 7)
    amplitudes = noise_with(key_of[0], (NI, NK, V, V), 1.0, 6.0, ((1, 4), (2, 8)), (3, 2, 8, 2.0))
    cycle_block = centred(key_of[1], (V, NK, NJ, V), (NK * V // 8) ** -0.5, 0.078125, ((0, 8), (2, 4)))
    occ_sizes = uneven(key_of[2], IRREPS, NK, NK // 4, 2).astype(jnp.int32)
    vir_sizes = uneven(key_of[3], IRREPS, V, V // 4, 2).astype(jnp.int32)
    window_i = with_ends(jax.random.randint(key_of[4], (NI,), 0, NK), jax.random.fold_in(key_of[4], 1), 0, NK - 1).astype(jnp.int32)
    window_occ = with_ends(jax.random.randint(key_of[5], (NJ,), 0, NK), jax.random.fold_in(key_of[5], 1), 0, NK - 1).astype(jnp.int32)
    return dict(amplitudes=amplitudes, cycle_block=cycle_block, occ_sizes=occ_sizes, vir_sizes=vir_sizes, window_i=window_i, window_occ=window_occ)


def irrep_labels(sizes, count):
    boundaries = jnp.cumsum(sizes).astype(jnp.int32)
    positions = jnp.arange(count, dtype=jnp.int32)
    return jnp.sum((positions[:, None] >= boundaries[None, :]).astype(jnp.int32), axis=1).astype(jnp.int32)


def reference(amplitudes, cycle_block, occ_sizes, vir_sizes, window_i, window_occ):
    occ_labels = irrep_labels(occ_sizes, NK)
    vir_labels = irrep_labels(vir_sizes, V)
    i_labels = occ_labels[window_i]
    amp_parity = jnp.bitwise_xor(
        jnp.bitwise_xor(i_labels[:, None, None, None], occ_labels[None, :, None, None]),
        jnp.bitwise_xor(vir_labels[None, None, :, None], vir_labels[None, None, None, :]))
    masked_amps = jnp.where(amp_parity == 0, amplitudes, jnp.zeros_like(amplitudes))
    left_matrix = jnp.transpose(masked_amps, (0, 2, 1, 3)).reshape(NI * V, NK * V)

    def one_column(column):
        column_slab = lax.dynamic_index_in_dim(cycle_block, column, 2, keepdims=False)
        j_label = occ_labels[window_occ[column]]
        parity = jnp.bitwise_xor(jnp.bitwise_xor(vir_labels[:, None, None], occ_labels[None, :, None]), jnp.bitwise_xor(j_label, vir_labels[None, None, :]))
        masked = jnp.where(parity == 0, column_slab, jnp.zeros_like(column_slab))
        right_matrix = jnp.transpose(masked, (1, 0, 2)).reshape(NK * V, V)
        return jnp.dot(left_matrix, right_matrix, preferred_element_type=jnp.float32).astype(jnp.bfloat16)

    results = lax.map(one_column, jnp.arange(NJ, dtype=jnp.int32))
    return jnp.transpose(results.reshape(NJ, NI, V, V), (1, 2, 0, 3))
```

```python
import jax
import jax.numpy as jnp
from jax import lax
from jax.sharding import PartitionSpec as P

FOLDS = 4


def irrep_labels(sizes, count):
    boundaries = jnp.cumsum(sizes)
    positions = jnp.arange(count, dtype=jnp.int32)
    return jnp.sum((positions[:, None] >= boundaries[None, :]).astype(jnp.int32), axis=1)


def label_lookup(orbitals, labels, count):
    matches = orbitals[:, None] == jnp.arange(count, dtype=jnp.int32)[None, :]
    return jnp.sum(jnp.where(matches, labels[None, :], 0), axis=1)


def body(n_pair, n_fold, amplitudes, cycle_block, occ_sizes, vir_sizes, window_i, window_occ):
    c_local, occ_total, j_local, vir_total = cycle_block.shape
    n_i, k_local, a_rows, _ = amplitudes.shape
    v_pack = vir_total // FOLDS
    k_pack = occ_total // FOLDS
    a_sub = a_rows // n_pair
    fold = lax.axis_index("fold")
    pair = lax.axis_index("pair")
    occ_labels = irrep_labels(occ_sizes, occ_total)
    vir_labels = irrep_labels(vir_sizes, vir_total)
    c_labels = lax.dynamic_slice_in_dim(vir_labels, fold * c_local, c_local)
    a_labels = lax.dynamic_slice_in_dim(vir_labels, fold * a_rows, a_rows)
    k_labels = lax.dynamic_slice_in_dim(occ_labels, pair * k_local, k_local)
    i_labels = label_lookup(window_i, occ_labels, occ_total)
    j_orbitals = lax.dynamic_slice_in_dim(window_occ, pair * j_local, j_local)
    j_labels = label_lookup(j_orbitals, occ_labels, occ_total)

    ika = i_labels[:, None, None] ^ k_labels[None, :, None] ^ a_labels[None, None, :]
    packed_c = 0
    for q in range(FOLDS):
        cut = slice(q * v_pack, (q + 1) * v_pack)
        keep = ika[..., None] == vir_labels[cut]
        packed_c = packed_c + jnp.where(keep, amplitudes[..., cut], 0)
    moved = lax.all_to_all(
        packed_c.reshape(n_i, k_local, n_pair, a_sub, v_pack), "pair", split_axis=2, concat_axis=1, tiled=True
    ).reshape(n_i, FOLDS, k_pack, a_sub, v_pack)
    own_a = lax.dynamic_slice_in_dim(a_labels, pair * a_sub, a_sub)
    ia = i_labels[:, None] ^ own_a[None, :]
    pieces = []
    for q in range(FOLDS):
        iac = ia[..., None] ^ vir_labels[q * v_pack:(q + 1) * v_pack]
        total = 0
        for s in range(FOLDS):
            keep = iac[:, None] == occ_labels[s * k_pack:(s + 1) * k_pack][None, :, None, None]
            total = total + jnp.where(keep, moved[:, s], 0)
        pieces.append(total)
    packed_k = jnp.concatenate(pieces, axis=-1)
    packed_k = packed_k.reshape(n_i, k_pack, a_sub, n_fold, c_local).transpose(3, 0, 2, 1, 4)
    packed_k = packed_k.reshape(n_fold, n_i * a_sub, k_pack * c_local)
    relaid = lax.all_to_all(packed_k, "fold", split_axis=0, concat_axis=0, tiled=True)
    gathered = lax.all_gather(relaid, "pair", axis=0, tiled=False)

    ckj = c_labels[:, None, None] ^ occ_labels[None, :, None] ^ j_labels[None, None, :]
    packed_w = 0
    for q in range(FOLDS):
        cut = slice(q * v_pack, (q + 1) * v_pack)
        keep = ckj[..., None] == vir_labels[cut]
        packed_w = packed_w + jnp.where(keep, cycle_block[..., cut], 0)
    packed_w = packed_w.reshape(c_local, FOLDS, k_pack, j_local * v_pack).transpose(1, 2, 0, 3)
    packed_w = packed_w.reshape(FOLDS, k_pack * c_local, j_local * v_pack)

    row_a = vir_labels.reshape(n_fold, n_pair, a_sub).transpose(1, 0, 2)
    row_labels = (row_a[:, :, None, :] ^ i_labels[:, None]).reshape(n_pair, n_fold, n_i * a_sub)
    partial_sum = 0
    for s in range(FOLDS):
        col_labels = (occ_labels[s * k_pack:(s + 1) * k_pack][:, None] ^ c_labels[None, :]).reshape(-1)
        lhs = jnp.where(row_labels[..., None] == col_labels, gathered, 0)
        partial_sum = partial_sum + jnp.einsum(
            "pfrx,xn->fprn", lhs, packed_w[s], preferred_element_type=jnp.float32
        )
    flat = partial_sum.reshape(-1, j_local * v_pack)
    own = lax.psum_scatter(flat, "fold", scatter_dimension=0, tiled=True)
    own = own.astype(jnp.bfloat16).reshape(n_pair, n_i, a_sub, j_local, v_pack)
    own = own.transpose(1, 0, 2, 3, 4).reshape(n_i, a_rows, j_local, v_pack)
    iaj = i_labels[:, None, None] ^ a_labels[None, :, None] ^ j_labels[None, None, :]
    keep = iaj[..., None] == vir_labels
    return jnp.where(keep, jnp.concatenate([own] * FOLDS, axis=-1), 0)


def solution(mesh):
    sizes = mesh.shape["pair"], mesh.shape["fold"]
    placed = (P(None, "pair", "fold", None), P("fold", None, "pair", None), P(), P(), P(), P())

    def run(*args):
        return body(*sizes, *args)

    return jax.shard_map(
        run, mesh=mesh, in_specs=placed, out_specs=P(None, "fold", "pair", None), check_vma=False
    )
```

```python
import functools

import jax
import jax.numpy as jnp
from jax import lax
from jax.experimental import pallas as pl
from jax.experimental.pallas import tpu as pltpu
from jax.sharding import PartitionSpec as P

LANES = 128
EARLY = 2
FOLDS = 4


def irrep_labels(sizes, count):
    boundaries = jnp.cumsum(sizes)
    positions = jnp.arange(count, dtype=jnp.int32)
    return jnp.sum((positions[:, None] >= boundaries[None, :]).astype(jnp.int32), axis=1)


def label_lookup(orbitals, labels, count):
    matches = orbitals[:, None] == jnp.arange(count, dtype=jnp.int32)[None, :]
    return jnp.sum(jnp.where(matches, labels[None, :], 0), axis=1)


def multiply_kernel(lhs_ref, *refs):
    rhs_refs, (row_ref, col_ref, out_ref) = refs[:FOLDS], refs[FOLDS:]
    n_pair = lhs_ref.shape[0]
    j_local = rhs_refs[0].shape[0]
    rows = row_ref[0].astype(jnp.bfloat16)
    left = jnp.concatenate([lhs_ref[p, 0] for p in range(n_pair)], axis=0)
    totals = [None] * j_local
    for s in range(FOLDS):
        keep = rows == col_ref[s].astype(jnp.bfloat16)
        part = jnp.where(keep, left, jnp.zeros_like(left))
        for j in range(j_local):
            term = jnp.dot(part, rhs_refs[s][j], preferred_element_type=jnp.float32)
            totals[j] = term if s == 0 else totals[j] + term
    for j, total in enumerate(totals):
        count, width = total.shape
        rest = width - LANES
        step = count * rest // LANES
        base = j * (count + step)
        out_ref[0, base:base + count] = total[:, :LANES]
        out_ref[0, base + count:base + count + step] = jnp.concatenate(
            [total[t * step:(t + 1) * step, LANES:] for t in range(LANES // rest)], axis=1
        )


def multiply(gathered, packed_w, row_labels, col_labels):
    n_pair, n_fold, span, depth = gathered.shape
    j_local, _, width = packed_w[0].shape
    rows = n_pair * span
    lines = j_local * rows * width // LANES
    rhs_spec = pl.BlockSpec(packed_w[0].shape, lambda f: (0, 0, 0), pipeline_mode=pl.Buffered(1))
    return pl.pallas_call(
        multiply_kernel,
        grid=(n_fold,),
        out_shape=jax.ShapeDtypeStruct((n_fold, lines, LANES), jnp.float32),
        in_specs=[pl.BlockSpec((n_pair, 1, span, depth), lambda f: (0, f, 0, 0))]
        + [rhs_spec] * FOLDS
        + [
            pl.BlockSpec((1, rows, 1), lambda f: (f, 0, 0)),
            pl.BlockSpec(col_labels.shape, lambda f: (0, 0, 0)),
        ],
        out_specs=pl.BlockSpec((1, lines, LANES), lambda f: (f, 0, 0)),
        compiler_params=pltpu.CompilerParams(vmem_limit_bytes=48 << 20),
        cost_estimate=pl.CostEstimate(
            flops=2 * n_fold * rows * FOLDS * depth * j_local * width,
            bytes_accessed=2 * gathered.size + 2 * FOLDS * packed_w[0].size,
            transcendentals=0,
        ),
    )(gathered, *packed_w, row_labels, col_labels)


def refold_kernel(occ_ref, moved_ref, row_ref, vir_ref, out_ref, wide_ref):
    n_pair, n_i, k_local, a_sub, v_pack = moved_ref.shape
    here, _, depth = out_ref.shape
    c_local = v_pack // here
    k_pack = depth // c_local
    for i in range(n_i):
        labels = row_ref[i] ^ vir_ref[0]
        for kappa in range(k_pack):
            total = jnp.zeros((a_sub, v_pack), jnp.float32)
            for s in range(FOLDS):
                k = s * k_pack + kappa
                piece = moved_ref[k // k_local, i, k % k_local].astype(jnp.float32)
                total = jnp.where(labels == occ_ref[k], piece, total)
            for f in range(here):
                wide_ref[f, i * a_sub:(i + 1) * a_sub, kappa * c_local:(kappa + 1) * c_local] = (
                    total[:, f * c_local:(f + 1) * c_local]
                )
    out_ref[...] = wide_ref[...].astype(out_ref.dtype)


def refold(moved, row_labels, vir_labels, occ_labels, c_local):
    _, n_i, _, a_sub, v_pack = moved.shape
    here = v_pack // c_local
    shape = (FOLDS * here, n_i * a_sub, occ_labels.shape[0] // FOLDS * c_local)
    return pl.pallas_call(
        refold_kernel,
        grid=(FOLDS,),
        out_shape=jax.ShapeDtypeStruct(shape, moved.dtype),
        in_specs=[
            pl.BlockSpec(memory_space=pltpu.SMEM),
            pl.BlockSpec(moved.shape, lambda q: (0, 0, 0, 0, 0), pipeline_mode=pl.Buffered(1)),
            pl.BlockSpec((n_i, a_sub, 1), lambda q: (0, 0, 0)),
            pl.BlockSpec((1, 1, v_pack), lambda q: (q, 0, 0)),
        ],
        out_specs=pl.BlockSpec((here,) + shape[1:], lambda q: (q, 0, 0)),
        scratch_shapes=[pltpu.VMEM((here,) + shape[1:], jnp.float32)],
        compiler_params=pltpu.CompilerParams(vmem_limit_bytes=40 << 20),
    )(occ_labels, moved, row_labels[..., None], vir_labels.reshape(FOLDS, 1, v_pack))


def body(n_pair, n_fold, amplitudes, cycle_block, occ_sizes, vir_sizes, window_i, window_occ):
    c_local, occ_total, j_local, vir_total = cycle_block.shape
    n_i, k_local, a_rows, _ = amplitudes.shape
    v_pack = vir_total // FOLDS
    k_pack = occ_total // FOLDS
    a_sub = a_rows // n_pair
    fold = lax.axis_index("fold")
    pair = lax.axis_index("pair")
    occ_labels = irrep_labels(occ_sizes, occ_total)
    vir_labels = irrep_labels(vir_sizes, vir_total)
    c_labels = lax.dynamic_slice_in_dim(vir_labels, fold * c_local, c_local)
    a_labels = lax.dynamic_slice_in_dim(vir_labels, fold * a_rows, a_rows)
    k_labels = lax.dynamic_slice_in_dim(occ_labels, pair * k_local, k_local)
    i_labels = label_lookup(window_i, occ_labels, occ_total)
    j_orbitals = lax.dynamic_slice_in_dim(window_occ, pair * j_local, j_local)
    j_labels = label_lookup(j_orbitals, occ_labels, occ_total)

    ika = i_labels[:, None, None] ^ k_labels[None, :, None] ^ a_labels[None, None, :]
    packed_c = 0
    for q in range(FOLDS):
        cut = slice(q * v_pack, (q + 1) * v_pack)
        keep = ika[..., None] == vir_labels[cut]
        packed_c = packed_c + jnp.where(keep, amplitudes[..., cut], 0)
    parts = packed_c.reshape(n_i, k_local, n_pair, a_sub, v_pack).transpose(2, 0, 1, 3, 4)
    moved = lax.all_to_all(parts, "pair", split_axis=0, concat_axis=0, tiled=True)
    depth = k_pack * c_local
    def pack_slices(source, wanted):
        made = []
        for s in wanted:
            block = source[:, s * k_pack:(s + 1) * k_pack].transpose(2, 1, 0, 3)
            own_k = occ_labels[s * k_pack:(s + 1) * k_pack]
            jkc = j_labels[:, None, None] ^ own_k[None, :, None] ^ c_labels[None, None, :]
            folded = 0
            for q in range(FOLDS):
                cut = slice(q * v_pack, (q + 1) * v_pack)
                keep = jkc[..., None] == vir_labels[cut]
                folded = folded + jnp.where(keep, block[..., cut], 0)
            made.append(folded.reshape(j_local, depth, v_pack))
        return made

    early = pack_slices(cycle_block, range(EARLY))
    moved, *early = lax.optimization_barrier((moved, *early))
    own_a = lax.dynamic_slice_in_dim(a_labels, pair * a_sub, a_sub)
    packed_k = refold(moved, i_labels[:, None] ^ own_a[None, :], vir_labels, occ_labels, c_local)
    packed_k, source = lax.optimization_barrier((packed_k, cycle_block))
    packed_w = list(early) + pack_slices(source, range(EARLY, FOLDS))
    relaid = lax.all_to_all(packed_k, "fold", split_axis=0, concat_axis=0, tiled=True)
    gathered = lax.all_gather(relaid, "pair", axis=0, tiled=False)

    row_a = vir_labels.reshape(n_fold, n_pair, a_sub)
    row_labels = (row_a[:, :, None, :] ^ i_labels[:, None]).reshape(n_fold, -1, 1)
    col_labels = (occ_labels[:, None] ^ c_labels[None, :]).reshape(FOLDS, 1, depth)
    count = n_pair * n_i * a_sub
    rest = v_pack - LANES
    step = count * rest // LANES
    partial_sum = multiply(gathered, packed_w, row_labels, col_labels)
    summed = lax.psum_scatter(
        partial_sum.reshape(-1, LANES), "fold", scatter_dimension=0, tiled=True
    ).astype(jnp.bfloat16)
    columns = []
    for j in range(j_local):
        own = summed[j * (count + step):(j + 1) * (count + step)]
        tail = jnp.concatenate(
            [own[count:, t * rest:(t + 1) * rest] for t in range(LANES // rest)], axis=0
        )
        columns.append(jnp.concatenate([own[:count], tail], axis=1))
    own = jnp.stack(columns, axis=1).reshape(n_pair, n_i, a_sub, j_local, v_pack)
    own = own.transpose(1, 0, 2, 3, 4).reshape(n_i, a_rows, j_local, v_pack)
    iaj = i_labels[:, None, None] ^ a_labels[None, :, None] ^ j_labels[None, None, :]
    keep = iaj[..., None] == vir_labels
    return jnp.where(keep, jnp.concatenate([own] * FOLDS, axis=-1), 0)


def solution(mesh):
    sizes = mesh.shape["pair"], mesh.shape["fold"]
    placed = (P(None, "pair", "fold", None), P("fold", None, "pair", None), P(), P(), P(), P())

    def run(*args):
        return body(*sizes, *args)

    return jax.shard_map(
        run, mesh=mesh, in_specs=placed, out_specs=P(None, "fold", "pair", None), check_vma=False
    )
```
